32 devices in a mesh: row: 8 (over z, x), col: 4 (over y, core).
Axes of the slice: x: 2, y: 2, z: 4, core: 2. Of those that a mesh axis runs over, the one named last changes fastest.
Arguments:
- x_window: bfloat16 [3, 2048, 512], P(None, 'row', 'col'), may hold values from -6 to 6
- y_window: float32 [3, 2048], P(None, 'row'), may hold values from -6 to 6
- block_order: int32 [3], replicated, may hold values from 0 to 2, each once
- diag_inverse: bfloat16 [3, 2048, 2048], P(None, 'row'), may hold values from -0.5 to 1.5, as said below
- panel_window: bfloat16 [3, 2048, 2048], P(None, 'row', 'col'), may hold values from -0.078125 to 0.078125
- panel_trail: bfloat16 [1024, 3, 2048], P('row', None, 'col'), may hold values from -0.078125 to 0.078125
- x_trail: bfloat16 [1024, 512], P('row', 'col'), may hold values from -6 to 6
- y_trail: float32 [1024], P('row'), may hold values from -6 to 6
Outputs:
- whitened: bfloat16 [3, 2048, 512], P(None, 'row', 'col')
- white_resp: bfloat16 [3, 2048], P(None, 'row')
- trail_rhs: float32 [1024, 512], P('row', 'col')
- trail_resp: float32 [1024], P('row')
- normal_part: float32 [512, 512], P('row')
- right_part: float32 [512], P('row')
The draws below stay inside these ranges and needn't reach their ends.
Inputs may be any that keep to these rules, and one draw needn't show every extreme that they name: Each diag_inverse[s] is lower triangular with a positive diagonal.
All inputs are finite; a program needn't handle non-finite values.
Results may differ from the reference program's by a relative error of at most 0.014.
Values may be sent and summed in bfloat16 or wider, within the bound.
No kernel may reach another device: no remote copies, remote signals or barrier semaphores. Data moves between devices by JAX's collectives and lax.ppermute only.
A program may use at most 64 MiB of HBM per device.

```python
import math
import jax
import jax.numpy as jnp
from jax import lax

P_SIZE = 512
NB = 2048
S = 3
TRAIL = 1024
PAIRS = 3


def draw_diag_inverse(key, part):
    key_off, key_diag = jax.random.split(jax.random.fold_in(key, 11))
    rows = lax.broadcasted_iota(jnp.int32, (S, NB, NB), 1)
    columns = lax.broadcasted_iota(jnp.int32, (S, NB, NB), 2)
    below = jax.random.normal(key_off, (S, NB, NB), jnp.float32)
    below = jnp.clip(below * (0.6 / math.sqrt(NB)), -0.5, 0.5)
    middle = jax.random.uniform(key_diag, (S, NB, NB), jnp.float32, 0.625, 1.5)
    values = jnp.where(rows == columns, middle, jnp.where(columns < rows, below, 0.0))
    return values.astype(jnp.bfloat16)


def block_scale(stream_key, extent, pieces, smallest, top_value):
    factor_of = 1.0
    for position, parts in pieces:
        heights = jax.random.uniform(jax.random.fold_in(jax.random.fold_in(stream_key, 6), position), (parts,), jnp.float32, smallest / len(pieces), top_value / len(pieces))
        factor_of = factor_of * jnp.repeat(jnp.exp(heights), extent[position] // parts).reshape((-1,) + (1,) * (len(extent) - 1 - position))
    return factor_of


def bell_draw(key, extent, width, bound, cuts=(), kind=jnp.bfloat16):
    array = jax.random.normal(key, extent, jnp.float32) * width
    if len(cuts) > 0:
        array = block_scale(key, extent, cuts, -0.22, 0.18) * array
    return jnp.clip(array, min=-bound, max=bound).astype(kind)


def setup_inputs(seed: int = 0) -> dict:
    key_of = jax.random.split(jax.random.key(seed), 9)
    x_window = bell_draw(key_of[0], (S, NB, P_SIZE), 1.0, 6.0, ((1, 8), (2, 4)))
    y_window = bell_draw(key_of[1], (S, NB), 1.0, 6.0, ((1, 8),), jnp.float32)
    block_order = jax.random.permutation(key_of[2], S).astype(jnp.int32)
    diag_inverse = draw_diag_inverse(jax.random.fold_in(key_of[8], 71), 0)
    panel_window = bell_draw(key_of[4], (PAIRS, NB, NB), (S * NB) ** -0.5, 0.078125, ((1, 8), (2, 4)))
    panel_trail = bell_draw(key_of[5], (TRAIL, S, NB), (S * NB) ** -0.5, 0.078125, ((0, 8), (2, 4)))
    x_trail = bell_draw(key_of[6], (TRAIL, P_SIZE), 1.0, 6.0, ((0, 8), (1, 4)))
    y_trail = bell_draw(key_of[7], (TRAIL,), 1.0, 6.0, ((0, 8),), jnp.float32)
    return {"x_window": x_window, "y_window": y_window, "block_order": block_order, "diag_inverse": diag_inverse, "panel_window": panel_window, "panel_trail": panel_trail, "x_trail": x_trail, "y_trail": y_trail}


def reference(x_window, y_window, block_order, diag_inverse, panel_window, panel_trail, x_trail, y_trail):
    hp = lax.Precision.HIGHEST
    solved = []
    solved_resp = []
    for s in range(S):
        pending = lax.dynamic_index_in_dim(x_window, block_order[s], 0, keepdims=False).astype(jnp.float32)
        pending_resp = lax.dynamic_index_in_dim(y_window, block_order[s], 0, keepdims=False)
        for t in range(s):
            factor = panel_window[s * (s - 1) // 2 + t].astype(jnp.float32)
            pending = pending - jnp.dot(factor, solved[t].astype(jnp.float32), precision=hp)
            pending_resp = pending_resp - jnp.dot(factor, solved_resp[t].astype(jnp.float32), precision=hp)
        residual = pending.astype(jnp.bfloat16)
        resid_resp = pending_resp.astype(jnp.bfloat16)
        solved.append(jnp.dot(diag_inverse[s], residual, preferred_element_type=jnp.float32).astype(jnp.bfloat16))
        solved_resp.append(jnp.dot(diag_inverse[s], resid_resp, preferred_element_type=jnp.float32).astype(jnp.bfloat16))
    whitened = jnp.stack(solved)
    white_resp = jnp.stack(solved_resp)
    zall = whitened.astype(jnp.float32)
    wall = white_resp.astype(jnp.float32)

    def one_block(s, carry):
        total, total_resp = carry
        factor = lax.dynamic_index_in_dim(panel_trail, s, 1, keepdims=False).astype(jnp.float32)
        block = lax.dynamic_index_in_dim(zall, s, 0, keepdims=False)
        block_resp = lax.dynamic_index_in_dim(wall, s, 0, keepdims=False)
        total = total + jnp.dot(factor, block, precision=hp)
        total_resp = total_resp + jnp.dot(factor, block_resp, precision=hp)
        return total, total_resp

    start = (jnp.zeros((TRAIL, P_SIZE), jnp.float32), jnp.zeros((TRAIL,), jnp.float32))
    total, total_resp = lax.fori_loop(0, S, one_block, start)
    trail_rhs = x_trail.astype(jnp.float32) - total
    trail_resp = y_trail - total_resp
    flat = zall.reshape(S * NB, P_SIZE)
    flat_resp = wall.reshape(S * NB)
    normal_part = jnp.dot(flat.T, flat, precision=hp) / (S * NB)
    right_part = jnp.dot(flat.T, flat_resp, precision=hp) / (S * NB)
    return whitened, white_resp, trail_rhs, trail_resp, normal_part, right_part
```

```python
import functools

import jax
import jax.numpy as jnp
from jax import lax
from jax.experimental import pallas as pl
from jax.experimental.pallas import tpu as pltpu
from jax.sharding import PartitionSpec as P

BF16 = jnp.bfloat16
F32 = jnp.float32
PAD = 8
CONTRACT_LAST = (((1,), (1,)), ((), ()))


def dot_t(a, b):
    return lax.dot_general(a, b, CONTRACT_LAST, preferred_element_type=F32)


class Place:
    def __init__(self, row, col):
        self.row, self.col = row, col
        self.z, self.x, self.core = row // 2, row % 2, col % 2
        self.scalars = None


def call(kernel, name, place, operands, outs, scratch):
    arrays, layers = [], []
    for item in operands:
        array, index = item if isinstance(item, tuple) else (item, None)
        arrays.append(array)
        layers.append(index)

    def body(scalars, *refs):
        views = [r if n is None else r.at[n] for r, n in zip(refs, layers)]
        kernel(scalars, *views, *refs[len(layers) :])

    vmem = pl.BlockSpec(memory_space=pltpu.VMEM)
    return pl.pallas_call(
        body,
        in_specs=[pl.BlockSpec(memory_space=pltpu.SMEM)] + [vmem] * len(arrays),
        out_specs=[vmem] * len(outs),
        out_shape=outs,
        scratch_shapes=scratch,
        name=name,
    )(place.scalars, *arrays)


def contract_kernel(plan, counts, scalars, *refs):
    tiles_n, mats_n, has_base, me, block = counts
    place = Place(scalars[0], scalars[1])
    tiles, refs = refs[:tiles_n], refs[tiles_n:]
    mats, refs = refs[:mats_n], refs[mats_n:]
    base, refs = (refs[0], refs[1:]) if has_base else (None, refs)
    out, gathered = refs
    for k, tile in enumerate(tiles):
        at = pl.multiple_of((me(place) ^ k) * block, block)
        gathered[:, pl.ds(at, block)] = tile[...]
    for members, rows, out_at in plan:
        total = None
        for index, width, col_at in members:
            at = pl.multiple_of(col_at(place), width)
            part = dot_t(gathered[:, pl.ds(at, width)], mats[index][...])
            total = part if total is None else total + part
        at = pl.ds(pl.multiple_of(out_at(place), rows), rows)
        if base is not None:
            total = base[:, at] - total
        out[:, at] = total.astype(out.dtype)


def contract(name, place, tiles, me, groups, out_rows, base=None, dtype=BF16):
    height, block = tiles[0].shape
    mats, plan = [], []
    for members, rows, out_at in groups:
        listed = []
        for mat, width, col_at in members:
            listed.append((len(mats), width, col_at))
            mats.append(mat)
        plan.append((listed, rows, out_at))
    widths = [w for members, _, _ in plan for _, w, _ in members] + [r for _, r, _ in plan]
    if all(w % 128 == 0 for w in widths + [block]):
        counts = (len(tiles), len(mats), base is not None, me, block)
        return call(
            functools.partial(contract_kernel, plan, counts),
            name,
            place,
            list(tiles) + mats + ([base] if base is not None else []),
            [jax.ShapeDtypeStruct((height, out_rows), dtype)],
            [pltpu.VMEM((height, block * len(tiles)), BF16)],
        )[0]
    order = me(place) ^ jnp.arange(len(tiles))
    gathered = jnp.stack(tiles)[order].transpose(1, 0, 2).reshape(height, -1)
    out = jnp.zeros((height, out_rows), F32)
    for members, rows, out_at in plan:
        total = 0.0
        for index, width, col_at in members:
            mat = mats[index]
            mat = mat[0][mat[1]] if isinstance(mat, tuple) else mat
            total += dot_t(lax.dynamic_slice_in_dim(gathered, col_at(place), width, 1), mat)
        if base is not None:
            total = lax.dynamic_slice_in_dim(base, out_at(place), rows, 1) - total
        out = lax.dynamic_update_slice_in_dim(out, total, out_at(place), 1)
    return out.astype(dtype)


def partial_kernel(counts, scalars, *refs):
    planes, cols, blocks, layers, has_base = counts
    place = Place(scalars[0], scalars[1])
    tiles, refs = refs[: 2 * cols], refs[2 * cols :]
    resps, refs = refs[: len(layers)], refs[len(layers) :]
    factors, refs = refs[: len(layers)], refs[len(layers) :]
    base, refs = (refs[: 2 * planes], refs[2 * planes :]) if has_base else (None, refs)
    grams, trails, wide = refs[:planes], refs[planes : 2 * planes], refs[2 * planes]
    half = tiles[0].shape[-2]
    trail_rows = factors[0].shape[0]
    full = 2 * cols * half
    for n in range(len(layers)):
        for dx in range(2):
            for dc in range(cols):
                at = (place.col ^ dc) * (2 * half) + (place.x ^ dx) * half
                wide[n, pl.ds(pl.multiple_of(at, half), half), :] = tiles[dx * cols + dc][n]
    for k in range(planes):
        to = place.z ^ k
        gram, resp, trail, trail_resp = 0.0, 0.0, 0.0, 0.0
        for n in range(len(layers)):
            own = wide[n, pl.ds(pl.multiple_of(to * (2 * half) + place.x * half, half), half), :]
            gram += dot_t(own, wide[n])
            resp += dot_t(resps[n][...], own)
            block = wide[n, pl.ds(pl.multiple_of(to * (2 * half), 2 * half), 2 * half), :]
            trail += dot_t(factors[n][...], block)
            trail_resp += dot_t(resps[n][...], factors[n][...])
        if has_base:
            gram += base[k][:half, :]
            resp += base[k][half:, :half]
            trail += base[planes + k][:trail_rows, : 2 * half]
            trail_resp += base[planes + k][trail_rows:, :trail_rows]
        kind = grams[k].dtype
        grams[k][:half, :] = gram.astype(kind)
        grams[k][half:, :] = jnp.zeros((PAD, full), kind)
        grams[k][half:, :half] = resp.astype(kind)
        trails[k][:trail_rows, : 2 * half] = trail.astype(kind)
        trails[k][trail_rows:, :trail_rows] = trail_resp.astype(kind)


def partials(name, place, planes, cols, tiles, resps, factors, layers, base, dtype):
    half, block = tiles[0].shape[-2:]
    trail_rows = factors.shape[1]
    full = 2 * cols * half
    gram = jax.ShapeDtypeStruct((half + PAD, full), dtype)
    trail = jax.ShapeDtypeStruct((trail_rows + PAD, max(2 * half, trail_rows)), dtype)
    counts = (planes, cols, block, layers, base is not None)
    return call(
        functools.partial(partial_kernel, counts),
        name,
        place,
        list(tiles) + list(resps) + [(factors, n) for n in layers] + list(base or []),
        [gram] * planes + [trail] * planes,
        [pltpu.VMEM((len(layers), full, block), BF16)],
    )


def final_kernel(planes, scale, scalars, *refs):
    grams, trails = refs[:planes], refs[planes : 2 * planes]
    x_ref, y_ref, rhs, resp, normal, right = refs[2 * planes :]
    half = normal.shape[0]
    rows = rhs.shape[0]
    gram = sum(g[...].astype(F32) for g in grams)
    trail = sum(t[...].astype(F32) for t in trails)
    normal[...] = gram[:half] * scale
    right[...] = gram[half:] * scale
    rhs[...] = x_ref[...].astype(F32) - trail[:rows, : rhs.shape[1]]
    resp[...] = y_ref[...] - trail[rows:, :rows]


def shards(
    x_window, y_window, block_order, diag_inverse, panel_window, panel_trail, x_trail, y_trail
):
    steps, rows, own_cols = x_window.shape
    width = panel_window.shape[2]
    n_rows, n_cols = lax.axis_size("row"), lax.axis_size("col")
    planes = n_rows // 2
    place = Place(lax.axis_index("row"), lax.axis_index("col"))
    place.scalars = jnp.stack([place.row, place.col]).astype(jnp.int32)
    x, core = place.x, place.core
    half = own_cols // 2
    pair = 2 * rows
    total_rows = rows * n_rows

    def move(array, to):
        table = []
        for r in range(n_rows):
            for c in range(n_cols):
                tr, tc = to(r, c)
                table.append((r * n_cols + c, tr * n_cols + tc))
        return lax.ppermute(array, ("row", "col"), table)

    def flip(array, dr=0, dc=0):
        return move(array, lambda r, c: (r ^ dr, c ^ dc))

    def ordered(own, other, axis):
        return jnp.where(
            x == 0,
            jnp.concatenate([own, other], axis),
            jnp.concatenate([other, own], axis),
        )

    def stored(s):
        xs = lax.dynamic_index_in_dim(x_window, block_order[s], 0, keepdims=False).T
        ys = lax.dynamic_index_in_dim(y_window, block_order[s], 0, keepdims=True)
        return xs, ys

    x0, y0 = stored(0)
    first = jnp.concatenate([x0, y0.astype(BF16), jnp.zeros((PAD - 1, rows), BF16)], 0)
    first_tiles = [first] + [flip(first, dr=k) for k in range(1, n_rows)]

    def panel(array):
        pieces = {(0, 0): array}
        bit = n_cols // 2
        while bit > 1:
            pieces |= {(dx, dc ^ bit): flip(a, dc=bit) for (dx, dc), a in pieces.items()}
            bit //= 2
        pieces |= {(1, dc): flip(a, dr=1) for (dx, dc), a in pieces.items()}
        pieces |= {(dx, dc ^ 1): flip(a, dc=1) for (dx, dc), a in pieces.items()}
        return pieces

    panels = {}
    for s in range(1, steps):
        at = s * (s - 1) // 2
        got = panel(panel_window[at : at + s])
        for t in range(s):
            panels[s, t] = {key: (a, t) for key, a in got.items()}

    part = lax.dynamic_slice_in_dim(diag_inverse, core * (rows // 2), rows // 2, 1)[1:]
    part_same = flip(part, dr=1)
    part_other = flip(part_same, dc=1)

    bases = []
    sent, kept = [], []
    for s in range(1, steps):
        xs, ys = stored(s)
        high = ys.astype(BF16)
        low = (ys - high.astype(F32)).astype(BF16)
        zeros = jnp.zeros((PAD - 2, rows), BF16)
        other = lax.dynamic_slice_in_dim(xs, (1 - x) * half, half, 0)
        own = lax.dynamic_slice_in_dim(xs, x * half, half, 0)
        sent.append(jnp.concatenate([other, high, low, zeros], 0))
        kept.append(jnp.concatenate([own.astype(F32), ys, jnp.zeros((PAD - 1, rows), F32)], 0))
    got = flip(jnp.stack(sent), dr=1).astype(F32)
    for n in range(steps - 1):
        resp = got[n, half : half + 1] + got[n, half + 1 : half + 2]
        other = jnp.concatenate([got[n, :half], resp, jnp.zeros((PAD - 1, rows), F32)], 0)
        bases.append(ordered(kept[n], other, 1))

    trail_factor = move(panel_trail.transpose(1, 0, 2), lambda r, c: (2 * c + r % 2, r // 2))

    def spread(tile):
        return [tile] + [flip(tile, dr=2 * k) for k in range(1, planes)]

    def solve(s, tiles):
        n = s - 1
        groups = [
            ([((diag_inverse, s), total_rows, lambda p: 0)], rows, lambda p: p.x * rows),
            (
                [((part_same, n), total_rows, lambda p: 0)],
                rows // 2,
                lambda p: (1 - p.x) * rows + p.core * (rows // 2),
            ),
            (
                [((part_other, n), total_rows, lambda p: 0)],
                rows // 2,
                lambda p: (1 - p.x) * rows + (1 - p.core) * (rows // 2),
            ),
        ]
        return contract(f"solve{s}", place, tiles, lambda p: p.z, groups, pair)

    def update(s, t, tiles, base, dtype):
        groups = []
        for dx in range(2):
            members = [
                (panels[s, t][dx, dc], width, lambda p, dc=dc: (p.col ^ dc) * width)
                for dc in range(n_cols)
            ]
            groups.append((members, rows, lambda p, dx=dx: (p.x ^ dx) * rows))
        return contract(f"update{s}{t}", place, tiles, lambda p: p.z, groups, pair, base, dtype)

    whole0 = contract(
        "solve0",
        place,
        first_tiles,
        lambda p: p.row,
        [([((diag_inverse, 0), total_rows, lambda p: 0)], rows, lambda p: 0)],
        rows,
    )
    resp0 = whole0[own_cols:]
    give = jnp.concatenate([lax.dynamic_slice_in_dim(whole0, (1 - x) * half, half, 0), resp0], 0)
    keep = jnp.concatenate([lax.dynamic_slice_in_dim(whole0, x * half, half, 0), resp0], 0)
    solved = [ordered(keep, flip(give, dr=1), 1)]
    pending = list(bases)
    for s in range(1, steps):
        tiles = spread(solved[s - 1])
        residual = update(s, s - 1, tiles, pending[s - 1], BF16)
        for later in range(s + 1, steps):
            pending[later - 1] = update(later, s - 1, tiles, pending[later - 1], F32)
        solved.append(solve(s, spread(residual)))

    early = jnp.stack([t[:half] for t in solved[:-1]])
    pieces = {(0, 0): early}
    bit = 1
    while bit < n_cols:
        pieces |= {(dx, dc ^ bit): flip(a, dc=bit) for (dx, dc), a in pieces.items()}
        bit *= 2
    pieces |= {(1, dc): flip(a, dr=1) for (dx, dc), a in pieces.items()}
    early_tiles = [pieces[dx, dc] for dx in range(2) for dc in range(n_cols)]
    late = solved[-1][:half][None]
    late_tiles = [
        flip(late, dr=dx, dc=dc) if dx or dc else late for dx in range(2) for dc in range(n_cols)
    ]
    resps = [t[half:] for t in solved]
    early_sums = partials(
        "early", place, planes, n_cols, early_tiles, resps[:-1], trail_factor,
        tuple(range(steps - 1)), None, F32,
    )
    late_sums = partials(
        "late", place, planes, n_cols, late_tiles, resps[-1:], trail_factor,
        (steps - 1,), early_sums, BF16,
    )
    grams = [late_sums[0]] + [flip(late_sums[k], dr=2 * k) for k in range(1, planes)]
    trails = [
        move(late_sums[planes + k], lambda r, c, k=k: (2 * c + r % 2, (r // 2) ^ k))
        for k in range(planes)
    ]
    scale = 1.0 / (steps * total_rows)
    full = own_cols * n_cols
    trail_rows = x_trail.shape[0]
    trail_rhs, trail_resp, normal, right = call(
        functools.partial(final_kernel, planes, scale),
        "final",
        place,
        grams + trails + [x_trail, y_trail[None]],
        [
            jax.ShapeDtypeStruct((trail_rows, own_cols), F32),
            jax.ShapeDtypeStruct((PAD, trail_rows), F32),
            jax.ShapeDtypeStruct((half, full), F32),
            jax.ShapeDtypeStruct((PAD, full), F32),
        ],
        [],
    )

    outs = [whole0[:own_cols].T]
    resp_outs = [resp0[0]]
    for s in range(1, steps):
        other = early_tiles[n_cols][s] if s < steps - 1 else late_tiles[n_cols][0]
        both = ordered(solved[s][:half], other, 0)
        outs.append(lax.dynamic_slice_in_dim(both, x * rows, rows, 1).T)
        resp_outs.append(lax.dynamic_slice_in_dim(solved[s][half], x * rows, rows, 0))
    return (
        jnp.stack(outs),
        jnp.stack(resp_outs),
        trail_rhs,
        trail_resp[0],
        normal,
        right[0, :half],
    )


def solution(mesh):
    in_specs = (
        P(None, "row", "col"),
        P(None, "row"),
        P(),
        P(None, "row", None),
        P(None, "row", "col"),
        P("row", None, "col"),
        P("row", "col"),
        P("row"),
    )
    out_specs = (
        P(None, "row", "col"),
        P(None, "row"),
        P("row", "col"),
        P("row"),
        P("row", None),
        P("row"),
    )
    return jax.shard_map(shards, mesh=mesh, in_specs=in_specs, out_specs=out_specs, check_vma=False)
```

```python
import functools

import jax
import jax.numpy as jnp
from jax import lax
from jax.experimental import pallas as pl
from jax.experimental.pallas import tpu as pltpu
from jax.sharding import PartitionSpec as P

BF16 = jnp.bfloat16
F32 = jnp.float32
PAD = 8
SCRATCH_BYTES = 12 * 2**20


def dot_t(a, b):
    return lax.dot_general(a, b, (((1,), (1,)), ((), ())), preferred_element_type=F32)


def aligned_at(offset, size):
    return pl.ds(pl.multiple_of(offset, size), size)


class Place:
    def __init__(self, row, col):
        self.row, self.col = row, col
        self.z, self.x, self.core = row // 2, row % 2, col % 2


def call(kernel, name, scalars, arrays, outs):
    outs, scratch = outs
    vmem = pl.BlockSpec(memory_space=pltpu.VMEM)

    def body(place, *refs):
        kernel(Place(place[0], place[1]), place, *refs)

    return pl.pallas_call(
        body,
        in_specs=[pl.BlockSpec(memory_space=pltpu.SMEM)] + [vmem] * len(arrays),
        out_specs=[vmem] * len(outs),
        out_shape=[pltpu.VMEM(shape, dtype) for shape, dtype in outs],
        scratch_shapes=[pltpu.VMEM(shape, dtype) for shape, dtype in scratch],
        compiler_params=pltpu.CompilerParams(vmem_limit_bytes=SCRATCH_BYTES),
        name=name,
    )(scalars, *[pltpu.with_memory_space_constraint(a, pltpu.VMEM) for a in arrays])


def prep_kernel(place, scalars, x_ref, y_ref, send, keep, turned):
    steps, _, _ = x_ref.shape
    half, rows = send.shape[1] - PAD, send.shape[2]
    at = lax.broadcasted_iota(jnp.int32, (PAD, rows), 0)
    for s in range(steps):
        stored = scalars[2 + s]
        turned[...] = x_ref[stored].astype(F32).T
        y = jnp.broadcast_to(y_ref[pl.ds(stored, 1), :], (PAD, rows))
        high = y.astype(BF16).astype(F32)
        keep[s, :half, :] = turned[aligned_at(place.x * half, half), :]
        keep[s, half:, :] = jnp.where(at == 0, y, 0.0)
        send[s, :half, :] = turned[aligned_at((1 - place.x) * half, half), :].astype(BF16)
        low = jnp.where(at == 1, y - high, 0.0)
        send[s, half:, :] = jnp.where(at == 0, high, low).astype(BF16)


def merge_kernel(place, scalars, keep, got, first, *bases):
    steps, height, rows = keep.shape
    half = height - PAD
    mine = aligned_at(place.x * rows, rows)
    other = aligned_at((1 - place.x) * rows, rows)
    at = lax.broadcasted_iota(jnp.int32, (PAD, rows), 0)
    for s in range(steps):
        out = first if s == 0 else bases[s - 1]
        tail = got[s, half:, :].astype(F32)
        resp = jnp.where(at == 0, jnp.sum(tail, 0, keepdims=True), 0.0)
        out[:, mine] = keep[s].astype(out.dtype)
        out[:half, other] = got[s, :half, :].astype(out.dtype)
        out[half:, other] = resp.astype(out.dtype)


def gather_tiles(place, tiles, gathered):
    block = tiles[0].shape[1]
    for k, tile in enumerate(tiles):
        gathered[:, aligned_at((place.z ^ k) * block, block)] = tile[...]


def solve_kernel(counts, place, scalars, *refs):
    planes, layer, offsets, extra = counts
    tiles, inverse, refs = refs[:planes], refs[planes], refs[planes + 1 :]
    parts, refs = refs[: len(offsets)], refs[len(offsets) :]
    before, refs = refs[: extra - 1], refs[extra - 1 :] if extra else refs
    out, gathered, other = refs[0], refs[-2], refs[-1]
    rows = inverse.shape[1]
    gather_tiles(place, tiles, gathered)
    for part, (dc, n) in zip(parts, offsets):
        count = part.shape[1]
        other[aligned_at((place.col ^ dc) * count, count), :] = part[n]
    out[:, aligned_at(place.x * rows, rows)] = dot_t(gathered[...], inverse[layer]).astype(BF16)
    theirs = dot_t(gathered[...], other[...]).astype(BF16)
    out[:, aligned_at((1 - place.x) * rows, rows)] = theirs
    if extra:
        copies = refs[1]
        half = copies.shape[1]
        for n, tile in enumerate(before):
            copies[n] = tile[:half, :]
        for n in range(len(before), copies.shape[0]):
            copies[n] = out[:half, :]


def update_kernel(counts, place, scalars, *refs):
    planes, pieces = counts
    tiles, refs = refs[:planes], refs[planes:]
    base, out, gathered, total = refs[-4:]
    gather_tiles(place, tiles, gathered)
    total[...] = base[...]
    for index, lead, where in pieces:
        piece = refs[index]
        rows, width = piece.shape[-2:]
        dx, dc = where(place)
        columns = gathered[:, aligned_at((place.col ^ dc) * width, width)]
        at = aligned_at((place.x ^ dx) * rows, rows)
        total[:, at] = total[:, at] - dot_t(columns, piece[lead])
    out[...] = total[...].astype(out.dtype)


def partial_kernel(counts, place, scalars, *refs):
    planes, tiles, layers, n_factors, has_base, n_arrays = counts
    arrays, refs = refs[:n_arrays], refs[n_arrays:]
    resps, refs = refs[: len(layers)], refs[len(layers) :]
    factors, refs = refs[:n_factors], refs[n_factors:]
    base, refs = (refs[0], refs[1:]) if has_base else (None, refs)
    outs, wide, sums = refs[:-2], refs[-2], refs[-1]
    full, block = wide.shape[1:]
    half = arrays[0].shape[-2]
    trail_rows = factors[0].shape[1]
    own_cols = 2 * half
    height = resps[0].shape[0] - PAD
    packed = own_cols % 128 == 0
    for index, lead, where in tiles:
        x, col = where(place)
        at = aligned_at(col * own_cols + x * half, half)
        for n in range(len(layers)):
            wide[n, at, :] = arrays[index][lead(n)]
    sums[...] = base[...] if has_base else jnp.zeros(sums.shape, F32)
    for k in range(planes):
        to = place.z ^ k
        for n in range(len(layers)):
            own = wide[n, aligned_at(to * own_cols + place.x * half, half), :]
            sums[k, :half, :] += dot_t(own, wide[n])
            sums[k, half : half + PAD, :half] += dot_t(resps[n][height:, :], own)
    for dc, factor in enumerate(factors):
        k = place.z ^ place.col ^ dc
        for n, layer in enumerate(layers):
            columns = wide[n, aligned_at(place.col * own_cols, own_cols), :]
            trail = dot_t(factor[layer], columns)
            if packed:
                per = full // own_cols
                count = trail_rows // per
                for j in range(per):
                    piece = trail[j * count : (j + 1) * count]
                    lanes = slice(j * own_cols, (j + 1) * own_cols)
                    sums[k, half + PAD :, lanes] += piece
            else:
                sums[k, half + PAD :, :own_cols] += trail
            resp = dot_t(resps[n][height:, :], factor[layer])
            sums[k, half : half + PAD, 128 : 128 + trail_rows] += resp
    if len(outs) == 1:
        outs[0][...] = sums[...]
    else:
        for k, out in enumerate(outs):
            out[...] = sums[k].astype(out.dtype)


def final_kernel(scale, place, scalars, *refs):
    slots = refs[:-6]
    x_ref, y_ref, rhs, resp, normal, right = refs[-6:]
    half, full = normal.shape
    trail_rows, own_cols = rhs.shape
    total = slots[0][...].astype(F32)
    for slot in slots[1:]:
        total += slot[...].astype(F32)
    normal[...] = total[:half] * scale
    right[...] = total[half : half + 1, :half] * scale
    resp[...] = y_ref[...] - total[half : half + 1, 128 : 128 + trail_rows]
    trail = total[half + PAD :]
    if own_cols % 128 == 0:
        per = full // own_cols
        count = trail_rows // per
        for j in range(per):
            rows, lanes = slice(j * count, (j + 1) * count), slice(j * own_cols, (j + 1) * own_cols)
            rhs[rows, :] = x_ref[rows, :].astype(F32) - trail[:, lanes]
    else:
        rhs[...] = x_ref[...].astype(F32) - trail[:, :own_cols]


def white_kernel(counts, place, scalars, *refs):
    steps, last_x, first_x, cols = counts
    solved, refs = refs[:steps], refs[steps:]
    late, early, out, resp_out, turned = refs[0], refs[1:-3], refs[-3], refs[-2], refs[-1]
    half = late.shape[1]
    rows = out.shape[1]
    lanes = aligned_at(place.x * rows, rows)
    row_at = lax.broadcasted_iota(jnp.int32, (steps, rows), 0)
    resps = jnp.zeros((steps, rows), F32)
    for s in range(steps):
        if s < steps - 1:
            (a, i), (b, j) = last_x, first_x
            mine = early[a][i, s, :, lanes].astype(F32)
            theirs = early[b][j, s, :, lanes].astype(F32)
            other = jnp.where(place.core == 0, mine, theirs)
        else:
            other = late[(1 - place.x) * cols + place.col, :, lanes].astype(F32)
        turned[aligned_at(place.x * half, half), :] = solved[s][:half, lanes].astype(F32)
        turned[aligned_at((1 - place.x) * half, half), :] = other
        out[s] = turned[...].T.astype(BF16)
        resp = solved[s][half:, lanes].astype(F32)[:1]
        resps = jnp.where(row_at == s, jnp.broadcast_to(resp, (steps, rows)), resps)
    resp_out[...] = resps.astype(BF16)


def shards(
    x_window, y_window, block_order, diag_inverse, panel_window, panel_trail, x_trail, y_trail
):
    steps, rows, own_cols = x_window.shape
    width = panel_window.shape[2]
    n_rows, n_cols = lax.axis_size("row"), lax.axis_size("col")
    planes = n_rows // 2
    place = Place(lax.axis_index("row"), lax.axis_index("col"))
    x, core = place.x, place.core
    half = own_cols // 2
    height = half + PAD
    pair = 2 * rows
    total_rows = rows * n_rows
    full = own_cols * n_cols
    trail_rows = x_trail.shape[0]
    kernels = rows % 128 == 0 and half % 8 == 0
    scalars = jnp.concatenate([jnp.stack([place.row, place.col]), block_order]).astype(jnp.int32)

    def move(array, to):
        table = []
        for r in range(n_rows):
            for c in range(n_cols):
                tr, tc = to(r, c)
                table.append((r * n_cols + c, tr * n_cols + tc))
        return lax.ppermute(array, ("row", "col"), table)

    def flip(array, dr=0, dc=0):
        return move(array, lambda r, c: (r ^ dr, c ^ dc))

    def ordered(own, other, axis):
        return jnp.where(
            x == 0,
            jnp.concatenate([own, other], axis),
            jnp.concatenate([other, own], axis),
        )

    far = []
    bit = n_cols // 2
    while bit > 1:
        far.append((0, bit))
        bit //= 2
    hops = (far + [(1, 0)], [(1, 0)] + far)

    def label(index, which):
        dx = dc = 0
        for stage, (hx, hc) in enumerate(hops[which]):
            if index >> stage & 1:
                dx, dc = dx ^ hx, dc ^ hc
        return dx, dc

    def hop(array, stage):
        def to(r, c):
            hx, hc = hops[c % 2][stage]
            return r ^ hx, c ^ hc

        return move(array, to)

    def finish(start, stage):
        held = start
        for n in range(stage, len(hops[0])):
            held = held + [hop(jnp.concatenate(held, 0) if len(held) > 1 else held[0], n)]
            if n + 1 < len(hops[0]):
                held = [jnp.concatenate(held, 0)]
        return held + [flip(a, dc=1) for a in held]

    def piece_labels(arrays):
        listed = []
        own = len(arrays) // 2
        for side in range(2):
            index = 0
            for n in range(own):
                for lead in range(arrays[n].shape[0]):

                    def where(p, index=index, side=side):
                        (ax, ac), (bx, bc) = label(index, side), label(index, 1 - side)
                        dx = jnp.where(p.core == 0, ax, bx)
                        dc = jnp.where(p.core == 0, ac, bc) ^ side
                        return dx, dc

                    listed.append((side * own + n, lead, where))
                    index += 1
        return listed

    if kernels:
        send, keep = call(
            prep_kernel,
            "prep",
            scalars,
            [x_window, y_window],
            (
                [((steps, height, rows), BF16), ((steps, height, rows), F32)],
                [((own_cols, rows), F32)],
            ),
        )
    else:
        xs = x_window[block_order].transpose(0, 2, 1).astype(F32)
        ys = y_window[block_order][:, None]
        high = ys.astype(BF16).astype(F32)
        fill = jnp.zeros((steps, PAD - 1, rows), F32)
        keep = jnp.concatenate([lax.dynamic_slice_in_dim(xs, x * half, half, 1), ys, fill], 1)
        other = lax.dynamic_slice_in_dim(xs, (1 - x) * half, half, 1)
        send = jnp.concatenate([other, high, ys - high, fill[:, 1:]], 1).astype(BF16)
    got = flip(send, dr=1)
    if kernels:
        residual, *pending = call(
            merge_kernel,
            "merge",
            scalars,
            [keep, got],
            ([((height, pair), BF16)] + [((height, pair), F32)] * (steps - 1), []),
        )
    else:
        resp = got[:, half:].astype(F32).sum(1, keepdims=True)
        theirs = jnp.concatenate([got[:, :half].astype(F32), resp, fill], 1)
        both = ordered(keep, theirs, 2)
        residual, pending = both[0].astype(BF16), list(both[1:])

    part_rows = rows // n_cols

    def partner_rows(first, count):
        part = lax.dynamic_slice(
            diag_inverse, (first, place.col * part_rows, 0), (count, part_rows, total_rows)
        )
        pieces = {0: flip(part, dr=1)}
        bit = n_cols // 2
        while bit:
            pieces |= {dc ^ bit: flip(a, dc=bit) for dc, a in pieces.items()}
            bit //= 2
        return pieces

    partner = [(partner_rows(0, 1), 0)]
    panel_next = hop(panel_window, 0)
    panels = {}
    for s in range(1, steps):
        at = s * (s - 1) // 2
        both = jnp.stack([panel_window[at : at + s], panel_next[at : at + s]])
        got_panels = finish([both], 1)
        panels[s] = (got_panels, piece_labels(got_panels))
        if s == 1:
            later = partner_rows(1, steps - 1)
            partner += [(later, n) for n in range(steps - 1)]

    factor = move(panel_trail.transpose(1, 0, 2), lambda r, c: (2 * c + r % 2, r // 2))
    factors = {0: factor}
    bit = n_cols // 2
    while bit:
        factors |= {dc ^ bit: flip(a, dc=bit) for dc, a in factors.items()}
        bit //= 2
    factors = [factors[dc] for dc in range(n_cols)]

    def spread(tile):
        return [tile] + [flip(tile, dr=2 * k) for k in range(1, planes)]

    def joined(tiles):
        order = place.z ^ jnp.arange(planes)
        return jnp.stack(tiles)[order].transpose(1, 0, 2).reshape(height, -1)

    def solve(s, tiles, before=None, copies=0):
        parts, n = partner[s]
        listed = sorted(parts)
        if kernels:
            outs = [((height, pair), BF16)]
            if copies:
                outs.append(((copies, half, pair), BF16))
            counts = (planes, s, [(dc, n) for dc in listed], 1 + len(before) if copies else 0)
            return call(
                functools.partial(solve_kernel, counts),
                f"solve{s}",
                scalars,
                tiles + [diag_inverse] + [parts[dc] for dc in listed] + (before or []),
                (outs, [((height, total_rows), BF16), ((rows, total_rows), BF16)]),
            )
        order = place.col ^ jnp.arange(n_cols)
        other = jnp.stack([parts[dc][n] for dc in listed])[order].reshape(rows, total_rows)
        both = ordered(diag_inverse[s], other, 0)
        out = dot_t(joined(tiles), both).astype(BF16)
        copied = [t[:half] for t in before or []]
        copied += [out[:half]] * (copies - len(copied))
        return [out, jnp.stack(copied)] if copies else [out]

    def update(s, t, tiles, base, dtype):
        arrays, labels = panels[s]
        if kernels:
            counts = (planes, [(i, (lead, t), where) for i, lead, where in labels])
            return call(
                functools.partial(update_kernel, counts),
                f"update{s}{t}",
                scalars,
                tiles + arrays + [base],
                (
                    [((height, pair), dtype)],
                    [((height, total_rows), BF16), ((height, pair), F32)],
                ),
            )[0]
        gathered, total = joined(tiles), base
        for i, lead, where in labels:
            dx, dc = where(place)
            columns = lax.dynamic_slice_in_dim(gathered, (place.col ^ dc) * width, width, 1)
            at = (x ^ dx) * rows
            now = lax.dynamic_slice_in_dim(total, at, rows, 1)
            now = now - dot_t(columns, arrays[i][lead, t])
            total = lax.dynamic_update_slice_in_dim(total, now, at, 1)
        return total.astype(dtype)

    solved = []
    group = 2 * n_cols
    for s in range(steps):
        copied = None
        tiles = spread(residual)
        if s == steps - 1:
            tile, copied = solve(s, tiles, [], group)
        elif s == steps - 2:
            tile, copied = solve(s, tiles, list(solved), steps - 1)
        else:
            (tile,) = solve(s, tiles)
        solved.append(tile)
        if s == steps - 2:
            early = finish([copied[None]], 0)
        if s == steps - 1:
            table = [
                [r * n_cols + c for r in (2 * z, 2 * z + 1) for c in range(n_cols)]
                for z in range(planes)
            ]
            late = lax.all_to_all(
                copied, ("row", "col"), 0, 0, tiled=True, axis_index_groups=table
            )
        else:
            tiles = spread(tile)
            residual = update(s + 1, s, tiles, pending[s], BF16)
            for later in range(s + 2, steps):
                pending[later - 1] = update(later, s, tiles, pending[later - 1], F32)

    packed = own_cols % 128 == 0
    slot = half + PAD + (trail_rows * own_cols // full if packed else trail_rows)

    def partials(name, layers, arrays, tiles, resps, base, outs):
        counts = (planes, tiles, layers, n_cols, base is not None, len(arrays))
        return call(
            functools.partial(partial_kernel, counts),
            name,
            scalars,
            arrays + resps + factors + ([] if base is None else [base]),
            (outs, [((len(layers), full, pair), BF16), ((planes, slot, full), F32)]),
        )

    early_tiles = []
    for i, lead, where in piece_labels(early):

        def early_at(p, where=where):
            dx, dc = where(p)
            return p.x ^ dx, p.col ^ dc

        early_tiles.append((i, lambda n, lead=lead: (lead, n), early_at))
    late_tiles = [
        (0, lambda n, m=m: m, lambda p, m=m: (m // n_cols, m % n_cols)) for m in range(group)
    ]
    (sums,) = partials(
        "early", tuple(range(steps - 1)), early, early_tiles, solved[:-1], None,
        [((planes, slot, full), F32)],
    )
    slots = partials(
        "late", (steps - 1,), [late], late_tiles, solved[-1:], sums,
        [((slot, full), BF16)] * planes,
    )
    slots = [slots[0]] + [flip(slots[k], dr=2 * k) for k in range(1, planes)]
    scale = 1.0 / (steps * total_rows)
    trail_rhs, trail_resp, normal, right = call(
        functools.partial(final_kernel, scale),
        "final",
        scalars,
        slots + [x_trail, y_trail[None]],
        (
            [
                ((trail_rows, own_cols), F32),
                ((1, trail_rows), F32),
                ((half, full), F32),
                ((1, half), F32),
            ],
            [],
        ),
    )

    flat = [(n, i) for n in range(len(early) // 2) for i in range(early[n].shape[0])]
    last_x, first_x = flat[1 << (len(hops[0]) - 1)], flat[1]
    if kernels:
        whitened, white_resp = call(
            functools.partial(white_kernel, (steps, last_x, first_x, n_cols)),
            "white",
            scalars,
            solved + [late] + early[: len(early) // 2],
            (
                [((steps, rows, own_cols), BF16), ((steps, rows), BF16)],
                [((own_cols, rows), F32)],
            ),
        )
    else:
        outs, resps = [], []
        for s in range(steps):
            if s < steps - 1:
                (a, i), (b, j) = last_x, first_x
                other = jnp.where(core == 0, early[a][i, s], early[b][j, s])
            else:
                other = late[(1 - x) * n_cols + place.col]
            both = ordered(solved[s][:half], other, 0)
            outs.append(lax.dynamic_slice_in_dim(both, x * rows, rows, 1).T)
            resps.append(lax.dynamic_slice_in_dim(solved[s][half], x * rows, rows, 0))
        whitened, white_resp = jnp.stack(outs), jnp.stack(resps)
    return whitened, white_resp, trail_rhs, trail_resp[0], normal, right[0]


def solution(mesh):
    in_specs = (
        P(None, "row", "col"),
        P(None, "row"),
        P(),
        P(None, "row", None),
        P(None, "row", "col"),
        P("row", None, "col"),
        P("row", "col"),
        P("row"),
    )
    out_specs = (
        P(None, "row", "col"),
        P(None, "row"),
        P("row", "col"),
        P("row"),
        P("row", None),
        P("row"),
    )
    return jax.shard_map(shards, mesh=mesh, in_specs=in_specs, out_specs=out_specs, check_vma=False)
```

```python
import functools

import jax
import jax.numpy as jnp
from jax import lax
from jax.experimental import pallas as pl
from jax.experimental.pallas import tpu as pltpu
from jax.sharding import PartitionSpec as P


BF16 = jnp.bfloat16
F32 = jnp.float32
PAD = 8
SCRATCH_BYTES = 12 * 2**20


def dot_t(a, b):
    return lax.dot_general(a, b, (((1,), (1,)), ((), ())), preferred_element_type=F32)


def aligned_at(offset, size):
    return pl.ds(pl.multiple_of(offset, size), size)


class Place:
    def __init__(self, row, col):
        self.row, self.col = row, col
        self.z, self.x, self.core = row // 2, row % 2, col % 2


def here():
    return Place(lax.axis_index("row"), lax.axis_index("col"))


def call(kernel, arrays, outs, scratch=(), plain=(), hbm=(), more=(), to_hbm=False):
    vmem = pl.BlockSpec(memory_space=pltpu.VMEM)
    specs, given = [], []
    for n, array in enumerate(arrays):
        if n in hbm:
            specs.append(pl.BlockSpec(memory_space=pltpu.HBM))
            array = pltpu.with_memory_space_constraint(array, pltpu.HBM)
        elif n in plain:
            specs.append(vmem)
        else:
            specs.append(vmem)
            array = pltpu.with_memory_space_constraint(array, pltpu.VMEM)
        given.append(array)
    kind = jax.ShapeDtypeStruct if to_hbm else pltpu.VMEM
    return pl.pallas_call(
        lambda *refs: kernel(here(), *refs),
        in_specs=specs,
        out_specs=[vmem] * len(outs),
        out_shape=[kind(shape, dtype) for shape, dtype in outs],
        scratch_shapes=[pltpu.VMEM(shape, dtype) for shape, dtype in scratch]
        + list(more),
        compiler_params=pltpu.CompilerParams(vmem_limit_bytes=SCRATCH_BYTES),
    )(*given)


def parts_kernel(inverse, *refs):
    outs, sems = refs[:-1], refs[-1]
    place = here()
    block = inverse.shape[1]
    half, depth = outs[0].shape
    pieces = []
    for k in range(depth // block):
        columns = aligned_at((2 * k + 1 - place.x) * block, block)
        source = inverse.at[0, aligned_at(place.core * half, half), columns]
        pieces.append((source, outs[0].at[:, pl.ds(k * block, block)]))
    for n, out in enumerate(outs[1:]):
        rows = out.shape[1]
        source = inverse.at[n + 1, aligned_at(place.col * rows, rows), :]
        pieces.append((source, out.at[0]))
    copies = [
        pltpu.make_async_copy(source, target, sems.at[n])
        for n, (source, target) in enumerate(pieces)
    ]
    for copy in copies:
        copy.start()
    for copy in copies:
        copy.wait()


def pack_kernel(place, own, got, *outs):
    at = 0
    for out in outs:
        count = out.shape[1]
        out[0] = own[at : at + count]
        out[1] = got[at : at + count]
        at += count


def prep_kernel(place, order_hbm, x_hbm, y_hbm, first, send, keep, turned, *held):
    half, rows = send.shape[1] - PAD, send.shape[2]
    x_ref, y_ref, order, sems = held
    pairs = [(order_hbm, order), (x_hbm, x_ref), (y_hbm, y_ref)]
    copies = [pltpu.make_async_copy(a, b, sems.at[n]) for n, (a, b) in enumerate(pairs)]
    for copy in copies:
        copy.start()
    for copy in copies:
        copy.wait()
    at = lax.broadcasted_iota(jnp.int32, (PAD, rows), 0)
    for s in range(x_ref.shape[0]):
        stored = order[s]
        turned[...] = x_ref[stored].astype(F32).T
        y = jnp.broadcast_to(y_ref[pl.ds(stored, 1), :], (PAD, rows))
        high = y.astype(BF16).astype(F32)
        if s == 0:
            first[: 2 * half, :] = turned[...].astype(BF16)
            first[2 * half :, :] = jnp.where(at == 0, y, 0.0).astype(BF16)
            continue
        n = s - 1
        keep[n, :half, :] = turned[aligned_at(place.x * half, half), :]
        keep[n, half:, :] = jnp.where(at == 0, y, 0.0)
        send[n, :half, :] = turned[aligned_at((1 - place.x) * half, half), :].astype(BF16)
        low = jnp.where(at == 1, y - high, 0.0)
        send[n, half:, :] = jnp.where(at == 0, high, low).astype(BF16)


def merge_kernel(place, keep, got, *bases):
    _, height, rows = keep.shape
    half = height - PAD
    mine = aligned_at(place.x * rows, rows)
    other = aligned_at((1 - place.x) * rows, rows)
    at = lax.broadcasted_iota(jnp.int32, (PAD, rows), 0)
    for n, out in enumerate(bases):
        tail = got[n, half:, :].astype(F32)
        resp = jnp.where(at == 0, jnp.sum(tail, 0, keepdims=True), 0.0)
        out[:, mine] = keep[n]
        out[:half, other] = got[n, :half, :].astype(F32)
        out[half:, other] = resp


def join_kernel(place, keep, got, out):
    out[...] = (keep[...] + got[...].astype(F32)).astype(out.dtype)


def first_kernel(place, *refs):
    tiles, (inverse, mine, theirs, keep, send, gathered, total) = refs[:-7], refs[-7:]
    block = tiles[0].shape[1]
    half = keep.shape[0] - PAD
    rows = mine.shape[0]
    gather_tiles(place, tiles, gathered)
    own = None
    for k in range(len(tiles)):
        columns = aligned_at((2 * k + place.x) * block, block)
        part = dot_t(gathered[:, k * block : (k + 1) * block], inverse[0, :, columns])
        own = part if own is None else own + part
    total[:, aligned_at(place.x * block, block)] = own
    at = (1 - place.x) * block
    total[:, aligned_at(at + place.core * rows, rows)] = dot_t(gathered[...], mine[...])
    total[:, aligned_at(at + (1 - place.core) * rows, rows)] = dot_t(gathered[...], theirs[...])
    keep[:half, :] = total[aligned_at(place.x * half, half), :]
    keep[half:, :] = total[2 * half :, :]
    send[:half, :] = total[aligned_at((1 - place.x) * half, half), :].astype(BF16)
    send[half:, :] = total[2 * half :, :].astype(BF16)


def gather_tiles(place, tiles, gathered):
    block = tiles[0].shape[1]
    for k, tile in enumerate(tiles):
        gathered[:, aligned_at((place.z ^ k) * block, block)] = tile[...]


def solve_kernel(counts, place, *refs):
    planes, layer, offsets, befores = counts
    tiles, inverse, refs = refs[:planes], refs[planes], refs[planes + 1 :]
    parts, refs = refs[: len(offsets)], refs[len(offsets) :]
    before, outs, gathered, other = refs[:befores], refs[befores:-2], refs[-2], refs[-1]
    rows = inverse.shape[1]
    gather_tiles(place, tiles, gathered)
    for part, dc in zip(parts, offsets):
        count = part.shape[1]
        other[aligned_at((place.col ^ dc) * count, count), :] = part[0]
    own = dot_t(gathered[...], inverse[layer]).astype(BF16)
    theirs = dot_t(gathered[...], other[...]).astype(BF16)
    mine, yours = aligned_at(place.x * rows, rows), aligned_at((1 - place.x) * rows, rows)
    for out in outs:
        if out.ndim == 2:
            height = out.shape[0]
            first = own.shape[0] - height
            out[:, mine] = own[first:]
            out[:, yours] = theirs[first:]
        else:
            height = out.shape[1]
            for m, tile in enumerate(before):
                out[m] = tile[...]
            out[len(before), :, mine] = own[:height]
            out[len(before), :, yours] = theirs[:height]


def update_kernel(counts, place, *refs):
    planes, pieces, arrays, has_base, split = counts
    tiles, refs = refs[:planes], refs[planes:]
    given, refs = refs[:arrays], refs[arrays:]
    base, refs = (refs[0], refs[1:]) if has_base else (None, refs)
    outs, gathered, total = refs[:-2], refs[-2], refs[-1]
    gather_tiles(place, tiles, gathered)
    total[...] = base[...] if has_base else jnp.zeros(total.shape, F32)
    for index, lead, where in pieces:
        piece = given[index]
        rows, width = piece.shape[-2:]
        dx, dc = where(place)
        columns = gathered[:, aligned_at((place.col ^ dc) * width, width)]
        at = aligned_at((place.x ^ dx) * rows, rows)
        total[:, at] = total[:, at] - dot_t(columns, piece[lead])
    if split:
        rows = outs[0].shape[1]
        outs[0][...] = total[:, aligned_at(place.x * rows, rows)]
        outs[1][...] = total[:, aligned_at((1 - place.x) * rows, rows)]
    else:
        outs[0][...] = total[...].astype(outs[0].dtype)


def partial_kernel(counts, place, *refs):
    planes, tiles, layers, has_base, n_arrays, apart, half = counts
    arrays, refs = refs[:n_arrays], refs[n_arrays:]
    resps, refs = (refs[0], refs[1:]) if apart else (arrays[0], refs)
    base, refs = (refs[0], refs[1:]) if has_base else (None, refs)
    outs, wide, sums = refs[:-2], refs[-2], refs[-1]
    own_cols = 2 * half
    resps = [resps[...] if apart else resps[0, n][half:, :] for n in range(layers)]
    for index, lead, where in tiles:
        x, col = where(place)
        at = aligned_at(col * own_cols + x * half, half)
        for n in range(layers):
            wide[n, at, :] = arrays[index][lead(n)][:half, :]
    sums[...] = base[...] if has_base else jnp.zeros(sums.shape, F32)
    for k in range(planes):
        to = place.z ^ k
        for n in range(layers):
            own = wide[n, aligned_at(to * own_cols + place.x * half, half), :]
            sums[k, :half, :] += dot_t(own, wide[n])
            sums[k, half:, :half] += dot_t(resps[n], own)
    if len(outs) == 1:
        outs[0][...] = sums[...]
    else:
        for k, out in enumerate(outs):
            out[...] = sums[k].astype(out.dtype)


def final_kernel(scale, place, *refs):
    slots = refs[:-8]
    mine, theirs, x_ref, y_ref, rhs, resp, normal, right = refs[-8:]
    half = normal.shape[0]
    total = slots[0][...].astype(F32)
    for slot in slots[1:]:
        total += slot[...].astype(F32)
    normal[...] = total[:half] * scale
    right[...] = total[half, :half] * scale
    resp[...] = y_ref[...] + mine[half, :]
    own, other = mine[:half, :].T, theirs[:half, :].T
    swapped = place.x == 1
    left, after = jnp.where(swapped, other, own), jnp.where(swapped, own, other)
    rhs[...] = x_ref[...].astype(F32) + jnp.concatenate([left, after], 1)


def white_kernel(counts, place, *refs):
    steps, last_x, first_x, n_early = counts
    early, late, (resp_ref, out, resp_out, turned) = refs[:n_early], refs[n_early:-4], refs[-4:]
    half = late[0].shape[-2]
    rows = out.shape[1]
    lanes = aligned_at(place.x * rows, rows)
    row_at = lax.broadcasted_iota(jnp.int32, (steps, rows), 0)
    resps = jnp.zeros((steps, rows), F32)
    (a, i), (b, j) = last_x, first_x
    for s in range(steps):
        arrays = early if s < steps - 1 else late
        n = s if s < steps - 1 else 0
        own = arrays[0][0, n, :, lanes]
        one = arrays[a][i, n, :half, lanes].astype(F32)
        two = arrays[b][j, n, :half, lanes].astype(F32)
        resp = own[half:] if s < steps - 1 else resp_ref[:, lanes]
        turned[aligned_at(place.x * half, half), :] = own[:half].astype(F32)
        other = jnp.where(place.core == 0, one, two)
        turned[aligned_at((1 - place.x) * half, half), :] = other
        out[s] = turned[...].T.astype(BF16)
        spread = jnp.broadcast_to(resp.astype(F32)[:1], (steps, rows))
        resps = jnp.where(row_at == s, spread, resps)
    resp_out[...] = resps.astype(BF16)


def shards(
    x_window, y_window, block_order, diag_inverse, panel_window, panel_trail, x_trail, y_trail
):
    steps, rows, own_cols = x_window.shape
    n_rows, n_cols = lax.axis_size("row"), lax.axis_size("col")
    planes = n_rows // 2
    place = here()
    x, core = place.x, place.core
    half = own_cols // 2
    height = half + PAD
    pair = 2 * rows
    total_rows = rows * n_rows
    full = own_cols * n_cols
    trail_rows = x_trail.shape[0]
    kernels = rows % 128 == 0 and half % 8 == 0

    def move(array, to):
        table = []
        for r in range(n_rows):
            for c in range(n_cols):
                tr, tc = to(r, c)
                table.append((r * n_cols + c, tr * n_cols + tc))
        return lax.ppermute(array, ("row", "col"), table)

    def flip(array, dr=0, dc=0):
        return move(array, lambda r, c: (r ^ dr, c ^ dc))

    def ordered(own, other, axis):
        return jnp.where(
            x == 0,
            jnp.concatenate([own, other], axis),
            jnp.concatenate([other, own], axis),
        )

    far = []
    bit = n_cols // 2
    while bit > 1:
        far.append((0, bit))
        bit //= 2
    hops = (far + [(1, 0)], [(1, 0)] + far)

    def label(index, which):
        dx = dc = 0
        for stage, (hx, hc) in enumerate(hops[which]):
            if index >> stage & 1:
                dx, dc = dx ^ hx, dc ^ hc
        return dx, dc

    def hop(array, stage):
        def to(r, c):
            hx, hc = hops[c % 2][stage]
            return r ^ hx, c ^ hc

        return move(array, to)

    def finish(start, stage):
        held = [start]
        for n in range(stage, len(hops[0])):
            held = held + [hop(held[0], n)]
            if n + 1 < len(hops[0]):
                held = [jnp.concatenate(held, 0)]
        return held + [flip(a, dc=1) for a in held]

    def piece_labels(arrays):
        listed = []
        own = len(arrays) // 2
        for side in range(2):
            index = 0
            for n in range(own):
                for lead in range(arrays[n].shape[0]):

                    def where(p, index=index, side=side):
                        (ax, ac), (bx, bc) = label(index, side), label(index, 1 - side)
                        dx = jnp.where(p.core == 0, ax, bx)
                        dc = jnp.where(p.core == 0, ac, bc) ^ side
                        return dx, dc

                    listed.append((side * own + n, lead, where))
                    index += 1
        return listed

    part_rows = rows // n_cols
    if kernels:
        sent_first, *sent_rows = pl.pallas_call(
            parts_kernel,
            in_specs=[pl.BlockSpec(memory_space=pltpu.HBM)],
            out_specs=[pl.BlockSpec(memory_space=pltpu.VMEM)] * steps,
            out_shape=[pltpu.VMEM((rows // 2, total_rows // 2), BF16)]
            + [pltpu.VMEM((1, part_rows, total_rows), BF16)] * (steps - 1),
            scratch_shapes=[pltpu.SemaphoreType.DMA((planes + steps - 1,))],
            compiler_params=pltpu.CompilerParams(vmem_limit_bytes=SCRATCH_BYTES),
            name="parts",
        )(pltpu.with_memory_space_constraint(diag_inverse, pltpu.HBM))
    else:
        cut = lax.dynamic_slice_in_dim(diag_inverse, place.col * part_rows, part_rows, 1)
        sent_rows = [cut[s : s + 1] for s in range(1, steps)]
        by_x = diag_inverse[0].reshape(rows, planes, 2, rows)
        sent_first = lax.dynamic_index_in_dim(by_x, 1 - x, 2, keepdims=False)
        sent_first = sent_first.reshape(rows, total_rows // 2)
        sent_first = lax.dynamic_slice_in_dim(sent_first, core * (rows // 2), rows // 2, 0)
    first_mine = flip(sent_first, dr=1)
    first_theirs = flip(first_mine, dc=1)

    def partner_rows(s):
        pieces = {0: flip(sent_rows[s - 1], dr=1)}
        bit = n_cols // 2
        while bit:
            for dc, a in list(pieces.items()):
                pieces[dc ^ bit] = flip(a, dc=bit)
            bit //= 2
        return pieces

    partner = {s: partner_rows(s) for s in range(1, steps)}

    if kernels:
        first, send, keep = call(
            prep_kernel,
            [block_order, x_window, y_window],
            [
                ((own_cols + PAD, rows), BF16),
                ((steps - 1, height, rows), BF16),
                ((steps - 1, height, rows), F32),
            ],
            [((own_cols, rows), F32), (x_window.shape, BF16), (y_window.shape, F32)],
            hbm=(0, 1, 2),
            more=[pltpu.SMEM(block_order.shape, jnp.int32), pltpu.SemaphoreType.DMA((3,))],
        )
    else:
        xs = x_window[block_order].transpose(0, 2, 1).astype(F32)
        ys = y_window[block_order][:, None]
        high = ys.astype(BF16).astype(F32)
        fill = jnp.zeros((steps, PAD - 1, rows), F32)
        first = jnp.concatenate([xs[0], ys[0], fill[0]], 0).astype(BF16)
        keep = jnp.concatenate([lax.dynamic_slice_in_dim(xs, x * half, half, 1), ys, fill], 1)
        other = lax.dynamic_slice_in_dim(xs, (1 - x) * half, half, 1)
        send = jnp.concatenate([other, high, ys - high, fill[:, 1:]], 1).astype(BF16)
        keep, send = keep[1:], send[1:]
    first_tiles = [first] + [flip(first, dr=2 * k) for k in range(1, planes)]
    got = flip(send, dr=1)
    if kernels:
        pending = list(call(merge_kernel, [keep, got], [((height, pair), F32)] * (steps - 1)))
    else:
        resp = got[:, half:].astype(F32).sum(1, keepdims=True)
        theirs = jnp.concatenate([got[:, :half].astype(F32), resp, fill[1:]], 1)
        pending = list(ordered(keep, theirs, 2))

    panel_next = hop(panel_window, 0)
    if kernels:
        packed_panels = call(
            pack_kernel,
            [panel_window, panel_next],
            [((2, s) + panel_window.shape[1:], BF16) for s in range(1, steps)],
        )
    else:
        packed_panels = []
        for s in range(1, steps):
            at = s * (s - 1) // 2
            packed_panels.append(jnp.stack([panel_window[at : at + s], panel_next[at : at + s]]))
    panels = {}
    for s in range(1, steps):
        got_panels = finish(packed_panels[s - 1], 1)
        panels[s] = (got_panels, piece_labels(got_panels))

    factors = finish(panel_trail.transpose(1, 0, 2)[None], 0)
    factor_labels = piece_labels(factors)

    def spread(tile):
        return [tile] + [flip(tile, dr=2 * k) for k in range(1, planes)]

    def joined(tiles):
        order = place.z ^ jnp.arange(planes)
        return jnp.stack(tiles)[order].transpose(1, 0, 2).reshape(tiles[0].shape[0], -1)

    def solve(s, tiles, before, outs):
        parts = partner[s]
        listed = sorted(parts)
        if kernels:
            return call(
                functools.partial(solve_kernel, (planes, s, listed, len(before))),
                tiles + [diag_inverse] + [parts[dc] for dc in listed] + before,
                [(shape, BF16) for shape in outs],
                [((height, total_rows), BF16), ((rows, total_rows), BF16)],
            )
        order = place.col ^ jnp.arange(n_cols)
        other = jnp.stack([parts[dc][0] for dc in listed])[order].reshape(rows, total_rows)
        both = ordered(diag_inverse[s], other, 0)
        out = dot_t(joined(tiles), both).astype(BF16)
        return [
            out[height - shape[0] :] if len(shape) == 2
            else jnp.stack(before + [out[: shape[1]]])
            for shape in outs
        ]

    def update(gathered_pieces, t, tiles, base, dtype, split=False):
        arrays, labels = gathered_pieces
        count, width = arrays[0].shape[-2:]
        if kernels:
            pieces = [(i, (lead, t), where) for i, lead, where in labels]
            counts = (planes, pieces, len(arrays), base is not None, split)
            shapes = [(height, count)] * 2 if split else [(height, 2 * count)]
            return call(
                functools.partial(update_kernel, counts),
                tiles + arrays + ([] if base is None else [base]),
                [(shape, dtype) for shape in shapes],
                [((height, total_rows), BF16), ((height, 2 * count), F32)],
            )
        gathered = joined(tiles)
        total = jnp.zeros((height, 2 * count), F32) if base is None else base
        for i, lead, where in labels:
            dx, dc = where(place)
            columns = lax.dynamic_slice_in_dim(gathered, (place.col ^ dc) * width, width, 1)
            at = (x ^ dx) * count
            now = lax.dynamic_slice_in_dim(total, at, count, 1)
            now = now - dot_t(columns, arrays[i][lead, t])
            total = lax.dynamic_update_slice_in_dim(total, now, at, 1)
        if split:
            return [
                lax.dynamic_slice_in_dim(total, side * count, count, 1) for side in (x, 1 - x)
            ]
        return [total.astype(dtype)]

    if kernels:
        keep0, send0 = call(
            first_kernel,
            first_tiles + [diag_inverse, first_mine, first_theirs],
            [((height, pair), F32), ((height, pair), BF16)],
            [((own_cols + PAD, total_rows // 2), BF16), ((own_cols + PAD, pair), F32)],
        )
        got0 = flip(send0, dr=1)
        (tile,) = call(join_kernel, [keep0, got0], [((height, pair), BF16)])
    else:
        own = lax.dynamic_index_in_dim(by_x, x, 2, keepdims=False).reshape(rows, -1)
        theirs = jnp.where(
            core == 0,
            jnp.concatenate([first_mine, first_theirs], 0),
            jnp.concatenate([first_theirs, first_mine], 0),
        )
        out = dot_t(joined(first_tiles), ordered(own, theirs, 0))
        resp = out[own_cols:]
        mine = lax.dynamic_slice_in_dim(out, x * half, half, 0)
        yours = lax.dynamic_slice_in_dim(out, (1 - x) * half, half, 0)
        got0 = flip(jnp.concatenate([yours, resp], 0).astype(BF16), dr=1)
        tile = (jnp.concatenate([mine, resp], 0) + got0.astype(F32)).astype(BF16)
    solved = []
    trail = None
    for s in range(steps):
        if s > 0:
            tiles = spread(residual)
        tile_shape = (height, pair)
        if s == steps - 1:
            shapes = [tile_shape, (1, half, pair), (PAD, pair)]
            tile, copied, late_resp = solve(s, tiles, [], shapes)
            late = finish(copied[None], 0)
        elif s == steps - 2:
            tile, copied = solve(s, tiles, solved, [tile_shape, (steps - 1, height, pair)])
            early = finish(copied[None], 0)
        elif s > 0:
            (tile,) = solve(s, tiles, [], [tile_shape])
        solved.append(tile)
        tiles = spread(tile)
        if s < steps - 1:
            (residual,) = update(panels[s + 1], s, tiles, pending[s], BF16)
        for later in range(s + 2, steps):
            (pending[later - 1],) = update(panels[later], s, tiles, pending[later - 1], F32)
        last = s == steps - 1
        trail = update((factors, factor_labels), s, tiles, trail, F32, last)
        trail = trail if last else trail[0]
    trail_mine, trail_sent = trail
    trail_got = flip(trail_sent, dr=1)

    def partials(layers, arrays, resp, base, outs):
        tiles = []
        for i, lead, where in piece_labels(arrays):

            def at(p, where=where):
                dx, dc = where(p)
                return p.x ^ dx, p.col ^ dc

            tiles.append((i, lambda n, lead=lead: (lead, n), at))
        has_base, apart = base is not None, resp is not None
        counts = (planes, tiles, layers, has_base, len(arrays), apart, half)
        more = ([resp] if apart else []) + ([base] if has_base else [])
        return call(
            functools.partial(partial_kernel, counts),
            arrays + more,
            outs,
            [((layers, full, pair), BF16), ((planes, height, full), F32)],
        )

    (sums,) = partials(steps - 1, early, None, None, [((planes, height, full), F32)])
    slots = partials(1, late, late_resp, sums, [((height, full), BF16)] * planes)
    slots = [slots[0]] + [flip(slots[k], dr=2 * k) for k in range(1, planes)]
    scale = 1.0 / (steps * total_rows)
    trail_rhs, trail_resp, normal, right = call(
        functools.partial(final_kernel, scale),
        slots + [trail_mine, trail_got, x_trail, y_trail],
        [
            ((trail_rows, own_cols), F32),
            ((trail_rows,), F32),
            ((half, full), F32),
            ((half,), F32),
        ],
        plain=(planes + 2, planes + 3),
        to_hbm=True,
    )

    own = len(early) // 2
    flat = [(n, i) for n in range(own) for i in range(early[n].shape[0])]
    last_x, first_x = flat[1 << (len(hops[0]) - 1)], flat[1]
    if kernels:
        whitened, white_resp = call(
            functools.partial(white_kernel, (steps, last_x, first_x, own)),
            early[:own] + late[:own] + [late_resp],
            [((steps, rows, own_cols), BF16), ((steps, rows), BF16)],
            [((own_cols, rows), F32)],
            to_hbm=True,
        )
    else:
        outs, resps = [], []
        (a, i), (b, j) = last_x, first_x
        for s in range(steps):
            arrays, n = (early, s) if s < steps - 1 else (late, 0)
            other = jnp.where(core == 0, arrays[a][i, n, :half], arrays[b][j, n, :half])
            both = ordered(arrays[0][0, n, :half], other, 0)
            resp = early[0][0, n, half] if s < steps - 1 else late_resp[0]
            outs.append(lax.dynamic_slice_in_dim(both, x * rows, rows, 1).T)
            resps.append(lax.dynamic_slice_in_dim(resp, x * rows, rows, 0))
        whitened, white_resp = jnp.stack(outs), jnp.stack(resps)
    return whitened, white_resp, trail_rhs, trail_resp, normal, right


def solution(mesh):
    in_specs = (
        P(None, "row", "col"),
        P(None, "row"),
        P(),
        P(None, "row", None),
        P(None, "row", "col"),
        P("row", None, "col"),
        P("row", "col"),
        P("row"),
    )
    out_specs = (
        P(None, "row", "col"),
        P(None, "row"),
        P("row", "col"),
        P("row"),
        P("row", None),
        P("row"),
    )

    return jax.shard_map(shards, mesh=mesh, in_specs=in_specs, out_specs=out_specs, check_vma=False)
```
